32 devices in a mesh: shard: 4 (over x, core), replica: 8 (over z, y).
Axes of the slice: x: 2, y: 2, z: 4, core: 2. Of those that a mesh axis runs over, the one named last changes fastest.
Arguments:
- layer_input: bfloat16 [8192, 1600], P(('shard', 'replica')), may hold values from -6 to 6
- norm1_gain: bfloat16 [1600], P('shard'), may hold values from 0.5 to 1.5
- norm1_shift: bfloat16 [1600], P('shard'), may hold values from -3 to 3
- qkv_weight: bfloat16 [1600, 4800], P('shard')
- query_bias: bfloat16 [1600], P('shard'), may hold values from -3 to 3
- value_bias: bfloat16 [1600], P('shard'), may hold values from -3 to 3
- out_weight: bfloat16 [1600, 1600], P('shard'), may hold values from -0.625 to 0.625
- out_bias: bfloat16 [1600], P('shard'), may hold values from -3 to 3
- norm2_gain: bfloat16 [1600], P('shard'), may hold values from 0.5 to 1.5
- norm2_shift: bfloat16 [1600], P('shard'), may hold values from -3 to 3
- fc_weight: bfloat16 [1600, 6400], P('shard'), may hold values from -0.15625 to 0.15625
- fc_bias: bfloat16 [6400], P('shard'), may hold values from -3 to 3
- proj_weight: bfloat16 [6400, 1600], P('shard'), may hold values from -0.078125 to 0.078125
- proj_bias: bfloat16 [1600], P('shard'), may hold values from -3 to 3
- cotangent: bfloat16 [8192, 1600], P(('shard', 'replica')), may hold values from -6 to 6
- seq_lengths: int32 [128], replicated, may hold values from 0 to 256, as said below
- seq_device: int32 [128], replicated, may hold values from 0 to 31, as said below
- seq_offset: int32 [128], replicated, may hold values from 0 to 256, as said below
Outputs:
- output: bfloat16 [8192, 1600], P(('shard', 'replica'))
- grad_x: bfloat16 [8192, 1600], P(('shard', 'replica'))
- grad_norm1_gain: float32 [1600], P('shard')
- grad_norm1_shift: float32 [1600], P('shard')
- grad_qkv_weight: float32 [1600, 4800], P('shard')
- grad_query_bias: float32 [1600], P('shard')
- grad_value_bias: float32 [1600], P('shard')
- grad_out_weight: float32 [1600, 1600], P('shard')
- grad_out_bias: float32 [1600], P('shard')
- grad_norm2_gain: float32 [1600], P('shard')
- grad_norm2_shift: float32 [1600], P('shard')
- grad_fc_weight: float32 [1600, 6400], P('shard')
- grad_fc_bias: float32 [6400], P('shard')
- grad_proj_weight: float32 [6400, 1600], P('shard')
- grad_proj_bias: float32 [1600], P('shard')
The draws below stay inside these ranges and needn't reach their ends.
Inputs may be any that keep to these rules, and one draw needn't show every extreme that they name: `seq_lengths`: some sequence has exactly 256 tokens; empty sequences occur. `seq_device`: device number = shard index * 8 + replica index; every device is named by exactly 4 sequences. The sequences of one device occupy disjoint ranges [seq_offset, seq_offset + seq_lengths) of its 256 positions.
All inputs are finite; a program needn't handle non-finite values.
Results may differ from the reference program's by a relative error of at most 0.018.
Values may be sent and summed in bfloat16 or wider, within the bound.
No kernel may reach another device: no remote copies, remote signals or barrier semaphores. Data moves between devices by JAX's collectives and lax.ppermute only.
A program may use at most 448 MiB of HBM per device.

```python
import math
import jax
import jax.numpy as jnp
from jax import lax

D = 1600
FF = 6400
HEAD = 64
TOK_DEV = 256
SEQ_DEV = 4
TOKENS = 8192
NSEQ = 128


def layout_tables(key):
    base = jax.random.fold_in(key, 7)
    keys = jax.random.split(base, 5)
    devices = NSEQ // SEQ_DEV
    fill = jax.random.randint(keys[0], (devices,), TOK_DEV // 2, TOK_DEV + 1)
    living = jax.random.randint(keys[1], (devices,), 1, SEQ_DEV + 1)
    chosen = jax.random.randint(keys[2], (), 0, devices)
    is_full = jnp.arange(devices, dtype=jnp.int32) == chosen
    fill = jnp.where(is_full, TOK_DEV, fill)
    living = jnp.where(is_full, 1, living)
    raw_cuts = jax.random.randint(keys[3], (devices, SEQ_DEV - 1), 0, 65536) % (fill[:, None] + 1)
    slot_index = jnp.arange(SEQ_DEV - 1, dtype=jnp.int32)
    cuts = jnp.where(slot_index[None, :] < living[:, None] - 1, raw_cuts, fill[:, None])
    cuts = jnp.sort(cuts, axis=1)
    bounds = jnp.concatenate([jnp.zeros((devices, 1), jnp.int32), cuts.astype(jnp.int32), fill[:, None].astype(jnp.int32)], axis=1)
    slot_lengths = (bounds[:, 1:] - bounds[:, :-1]).reshape(-1)
    slot_offsets = bounds[:, :-1].reshape(-1)
    order = jax.random.permutation(keys[4], NSEQ).astype(jnp.int32)
    return (slot_lengths[order].astype(jnp.int32), (order // SEQ_DEV).astype(jnp.int32), slot_offsets[order].astype(jnp.int32))


def draw_seq_lengths(key, part):
    return layout_tables(key)[0]


def draw_seq_device(key, part):
    return layout_tables(key)[1]


def draw_seq_offset(key, part):
    return layout_tables(key)[2]


def draw_qkv_weight(key, part):
    base = jax.random.normal(jax.random.fold_in(key, 11), (D, 3 * D), jnp.float32) / jnp.sqrt(jnp.float32(D))
    return base.astype(jnp.bfloat16)


def shard_levels(stream_key, shape, cuts, least, high):
    def one(axis_at, blocks):
        heights = jax.random.uniform(jax.random.fold_in(jax.random.fold_in(stream_key, 6), axis_at), (blocks,), jnp.float32, least / len(cuts), high / len(cuts))
        return jnp.repeat(jnp.exp(heights), shape[axis_at] // blocks).reshape((-1,) + (1,) * (len(shape) - axis_at - 1))

    factor_of = one(*cuts[0])
    for cut in cuts[1:]:
        factor_of = factor_of * one(*cut)
    return factor_of


def gaussian(own_key, extent, scale, limit, cuts=(), kind=jnp.bfloat16):
    gain = shard_levels(own_key, extent, cuts, -0.22, 0.18) if cuts else 1.0
    values = jax.random.normal(own_key, extent, jnp.float32) * scale * gain
    return jnp.minimum(jnp.maximum(values, -limit), limit).astype(kind)


def setup_inputs(seed: int = 0) -> dict:
    splits = jax.random.split(jax.random.key(seed), 19)
    return {
        "layer_input": gaussian(splits[0], (TOKENS, D), 1.0, 6.0, ((0, 32),)),
        "norm1_gain": jnp.clip(1.0 + 0.1 * jax.random.normal(splits[1], (D,), jnp.float32), 0.5, 1.5).astype(jnp.bfloat16),
        "norm1_shift": gaussian(splits[2], (D,), 0.5, 3.0, ((0, 4),)),
        "qkv_weight": draw_qkv_weight(jax.random.fold_in(splits[18], 71), 0),
        "query_bias": gaussian(splits[4], (D,), 0.5, 3.0, ((0, 4),)),
        "value_bias": gaussian(splits[5], (D,), 0.5, 3.0, ((0, 4),)),
        "out_weight": gaussian(splits[6], (D, D), (D // 16) ** -0.5, 0.625, ((0, 4),)),
        "out_bias": gaussian(splits[7], (D,), 0.5, 3.0, ((0, 4),)),
        "norm2_gain": jnp.clip(1.0 + 0.1 * jax.random.normal(splits[8], (D,), jnp.float32), 0.5, 1.5).astype(jnp.bfloat16),
        "norm2_shift": gaussian(splits[9], (D,), 0.5, 3.0, ((0, 4),)),
        "fc_weight": gaussian(splits[10], (D, FF), D ** -0.5, 0.15625, ((0, 4),)),
        "fc_bias": gaussian(splits[11], (FF,), 0.5, 3.0, ((0, 4),)),
        "proj_weight": gaussian(splits[12], (FF, D), FF ** -0.5, 0.078125, ((0, 4),)),
        "proj_bias": gaussian(splits[13], (D,), 0.5, 3.0, ((0, 4),)),
        "cotangent": gaussian(splits[14], (TOKENS, D), 1.0, 6.0, ((0, 32),)),
        "seq_lengths": draw_seq_lengths(jax.random.fold_in(splits[18], 71), 0),
        "seq_device": draw_seq_device(jax.random.fold_in(splits[18], 71), 0),
        "seq_offset": draw_seq_offset(jax.random.fold_in(splits[18], 71), 0),
    }


GELU_C = math.sqrt(2.0 / math.pi)

def normalize(values):
    centre = lax.optimization_barrier(jnp.mean(values, axis=-1, keepdims=True))
    shifted = values - centre
    spread = lax.optimization_barrier(jnp.mean(shifted * shifted, axis=-1, keepdims=True))
    inverse = lax.rsqrt(spread + 1e-05)
    return (shifted * inverse, inverse)

def norm_back(upstream, normed, inverse):
    first = lax.optimization_barrier(jnp.mean(upstream, axis=-1, keepdims=True))
    second = lax.optimization_barrier(jnp.mean(upstream * normed, axis=-1, keepdims=True))
    return inverse * (upstream - first - normed * second)

def gelu_pair(inputs):
    cubic = 0.044715 * inputs * inputs * inputs
    tangent = jnp.tanh(GELU_C * (inputs + cubic))
    value = 0.5 * inputs * (1.0 + tangent)
    slope = 0.5 * (1.0 + tangent) + 0.5 * inputs * (1.0 - tangent * tangent) * GELU_C * (1.0 + 3.0 * 0.044715 * inputs * inputs)
    return (value, slope)

def segment_ids(lengths, owners, offsets, device, count):
    position = jnp.arange(count, dtype=jnp.int32)
    number = jnp.arange(lengths.shape[0], dtype=jnp.int32)
    inside = (owners[:, None] == device) & (position[None, :] >= offsets[:, None]) & (position[None, :] < offsets[:, None] + lengths[:, None])
    owned = lax.optimization_barrier(jnp.sum(jnp.where(inside, number[:, None], 0), axis=0)).astype(jnp.int32)
    filled = jnp.any(inside, axis=0)
    return (jnp.where(filled, owned, -1 - position).astype(jnp.int32), filled)

def product(spec, left, right):
    return jnp.einsum(spec, left.astype(jnp.float32), right.astype(jnp.float32))

def mdot(left, right):
    return jnp.dot(left, right, preferred_element_type=jnp.float32)

def tdot(left, right):
    return jnp.dot(left.T, right, preferred_element_type=jnp.float32)

def ndot(left, right):
    return jnp.dot(left, right.T, preferred_element_type=jnp.float32)

def split_heads(packed, which):
    width_all = packed.shape[1] // 3
    return packed[:, which * width_all:(which + 1) * width_all].reshape(packed.shape[0], -1, HEAD)

def scores_of(packed, segment):
    query = split_heads(packed, 0)
    keys = split_heads(packed, 1)
    raw = product('qhd,khd->hqk', query, keys) * (1.0 / math.sqrt(HEAD))
    position = jnp.arange(packed.shape[0], dtype=jnp.int32)
    allowed = (segment[:, None] == segment[None, :]) & (position[None, :] <= position[:, None])
    return jnp.where(allowed[None], raw, -jnp.inf)

def forward(layer_input, segment, params):
    gain1, shift1, w_qkv, b_query, b_value, w_out, b_out, gain2, shift2, w_fc, b_fc, w_proj, b_proj = params
    count = layer_input.shape[0]
    inputs = layer_input.astype(jnp.float32)
    normed1, inverse1 = normalize(inputs)
    normed_in = (normed1 * gain1.astype(jnp.float32) + shift1.astype(jnp.float32)).astype(jnp.bfloat16)
    bias_all = jnp.concatenate([b_query.astype(jnp.float32), jnp.zeros(b_query.shape, jnp.float32), b_value.astype(jnp.float32)])
    packed = (mdot(normed_in, w_qkv) + bias_all).astype(jnp.bfloat16)
    scores = scores_of(packed, segment)
    highest = lax.optimization_barrier(jnp.max(scores, axis=-1, keepdims=True))
    expo = jnp.exp(scores - highest)
    total = lax.optimization_barrier(jnp.sum(expo, axis=-1, keepdims=True))
    probs = (expo / total).astype(jnp.bfloat16)
    logsum = highest + jnp.log(total)
    mixed = product('hqk,khd->qhd', probs, split_heads(packed, 2)).reshape(count, -1).astype(jnp.bfloat16)
    hidden = inputs + mdot(mixed, w_out) + b_out.astype(jnp.float32)
    normed2, inverse2 = normalize(hidden)
    mlp_in = (normed2 * gain2.astype(jnp.float32) + shift2.astype(jnp.float32)).astype(jnp.bfloat16)
    pre_act = mdot(mlp_in, w_fc) + b_fc.astype(jnp.float32)
    activ = gelu_pair(pre_act)[0].astype(jnp.bfloat16)
    result = (hidden + mdot(activ, w_proj) + b_proj.astype(jnp.float32)).astype(jnp.bfloat16)
    saved = (normed1, inverse1, normed_in, packed, mixed, logsum, segment, normed2, inverse2, mlp_in, pre_act, activ)
    return (result, saved)

def attend_back(packed, grad_mixed, logsum, segment):
    count = packed.shape[0]
    scores = scores_of(packed, segment)
    back_probs = jnp.exp(scores - logsum)
    probs_low = back_probs.astype(jnp.bfloat16)
    upstream = grad_mixed.reshape(count, -1, HEAD)
    query = split_heads(packed, 0)
    keys = split_heads(packed, 1)
    values = split_heads(packed, 2)
    grad_values = product('hqk,qhd->khd', probs_low, upstream)
    grad_probs = product('qhd,khd->hqk', upstream, values)
    delta = lax.optimization_barrier(jnp.sum(back_probs * grad_probs, axis=-1, keepdims=True))
    grad_scores = (back_probs * (grad_probs - delta) * (1.0 / math.sqrt(HEAD))).astype(jnp.bfloat16)
    grad_query = product('hqk,khd->qhd', grad_scores, keys)
    grad_keys = product('hqk,qhd->khd', grad_scores, query)
    return jnp.concatenate([grad_query.reshape(count, -1), grad_keys.reshape(count, -1), grad_values.reshape(count, -1)], axis=1)

def backward(cotangent, filled, saved, params):
    gain1, shift1, w_qkv, b_query, b_value, w_out, b_out, gain2, shift2, w_fc, b_fc, w_proj, b_proj = params
    normed1, inverse1, normed_in, packed, mixed, logsum, segment, normed2, inverse2, mlp_in, pre_act, activ = saved
    upstream = jnp.where(filled[:, None], cotangent.astype(jnp.float32), 0.0)
    upstream_low = upstream.astype(jnp.bfloat16)
    grad_wproj = tdot(activ, upstream_low)
    grad_bproj = lax.optimization_barrier(jnp.sum(upstream, axis=0))
    slope = gelu_pair(pre_act)[1]
    grad_pre = ndot(upstream_low, w_proj) * slope
    grad_pre_low = grad_pre.astype(jnp.bfloat16)
    grad_wfc = tdot(mlp_in, grad_pre_low)
    grad_bfc = lax.optimization_barrier(jnp.sum(grad_pre, axis=0))
    grad_mlp_in = ndot(grad_pre_low, w_fc)
    grad_gain2 = lax.optimization_barrier(jnp.sum(grad_mlp_in * normed2, axis=0))
    grad_shift2 = lax.optimization_barrier(jnp.sum(grad_mlp_in, axis=0))
    grad_hidden = upstream + norm_back(grad_mlp_in * gain2.astype(jnp.float32), normed2, inverse2)
    grad_bout = lax.optimization_barrier(jnp.sum(grad_hidden, axis=0))
    grad_hidden_low = grad_hidden.astype(jnp.bfloat16)
    grad_wout = tdot(mixed, grad_hidden_low)
    grad_mixed = ndot(grad_hidden_low, w_out).astype(jnp.bfloat16)
    grad_packed = attend_back(packed, grad_mixed, logsum, segment)
    width_all = w_out.shape[0]
    grad_bquery = lax.optimization_barrier(jnp.sum(grad_packed[:, :width_all], axis=0))
    grad_bvalue = lax.optimization_barrier(jnp.sum(grad_packed[:, 2 * width_all:], axis=0))
    grad_packed_low = grad_packed.astype(jnp.bfloat16)
    grad_wqkv = tdot(normed_in, grad_packed_low)
    grad_in = ndot(grad_packed_low, w_qkv)
    grad_gain1 = lax.optimization_barrier(jnp.sum(grad_in * normed1, axis=0))
    grad_shift1 = lax.optimization_barrier(jnp.sum(grad_in, axis=0))
    grad_inputs = (grad_hidden + norm_back(grad_in * gain1.astype(jnp.float32), normed1, inverse1)).astype(jnp.bfloat16)
    grads = (grad_gain1, grad_shift1, grad_wqkv, grad_bquery, grad_bvalue, grad_wout, grad_bout, grad_gain2, grad_shift2, grad_wfc, grad_bfc, grad_wproj, grad_bproj)
    return (grad_inputs, grads)

def reference(layer_input, norm1_gain, norm1_shift, qkv_weight, query_bias, value_bias, out_weight, out_bias, norm2_gain, norm2_shift, fc_weight, fc_bias, proj_weight, proj_bias, cotangent, seq_lengths, seq_device, seq_offset):
    params = (norm1_gain, norm1_shift, qkv_weight, query_bias, value_bias, out_weight, out_bias, norm2_gain, norm2_shift, fc_weight, fc_bias, proj_weight, proj_bias)
    blocks = TOKENS // TOK_DEV

    def step(carry, item):
        device, block_input, block_cot = item
        segment, filled = segment_ids(seq_lengths, seq_device, seq_offset, device, TOK_DEV)
        result, saved = forward(block_input, segment, params)
        grad_inputs, grads = backward(block_cot, filled, saved, params)
        return (tuple((left + right for left, right in zip(carry, grads))), (result, grad_inputs))
    start = tuple((jnp.zeros(param.shape, jnp.float32) for param in params))
    items = (jnp.arange(blocks, dtype=jnp.int32), layer_input.reshape(blocks, TOK_DEV, -1), cotangent.reshape(blocks, TOK_DEV, -1))
    sums, (results, grad_inputs) = lax.scan(step, start, items)
    return (results.reshape(TOKENS, -1), grad_inputs.reshape(TOKENS, -1), sums[0], sums[1], sums[2], sums[3], sums[4], sums[5], sums[6], sums[7], sums[8], sums[9], sums[10], sums[11], sums[12])
```

```python
import math

import jax
import jax.numpy as jnp
from jax import lax
from jax.sharding import PartitionSpec as P

HEAD = 64
LANES = 128
SUB = 8
AXES = ("shard", "replica")

GELU_C = math.sqrt(2.0 / math.pi)


def normalize(values):
    centre = jnp.mean(values, axis=-1, keepdims=True)
    shifted = values - centre
    spread = jnp.mean(shifted * shifted, axis=-1, keepdims=True)
    inverse = lax.rsqrt(spread + 1e-05)
    return (shifted * inverse, inverse)


def norm_back(upstream, normed, inverse):
    first = jnp.mean(upstream, axis=-1, keepdims=True)
    second = jnp.mean(upstream * normed, axis=-1, keepdims=True)
    return inverse * (upstream - first - normed * second)


def gelu_pair(inputs):
    cubic = 0.044715 * inputs * inputs * inputs
    tangent = jnp.tanh(GELU_C * (inputs + cubic))
    value = 0.5 * inputs * (1.0 + tangent)
    slope = 0.5 * (1.0 + tangent) + 0.5 * inputs * (1.0 - tangent * tangent) * GELU_C * (
        1.0 + 3.0 * 0.044715 * inputs * inputs
    )
    return (value, slope)


def segment_ids(lengths, owners, offsets, device, count):
    position = jnp.arange(count, dtype=jnp.int32)
    number = jnp.arange(lengths.shape[0], dtype=jnp.int32)
    inside = (
        (owners[:, None] == device)
        & (position[None, :] >= offsets[:, None])
        & (position[None, :] < offsets[:, None] + lengths[:, None])
    )
    owned = jnp.sum(jnp.where(inside, number[:, None], 0), axis=0)
    filled = jnp.any(inside, axis=0)
    return (jnp.where(filled, owned, -1 - position), filled)


def product(spec, left, right):
    return jnp.einsum(spec, left, right, preferred_element_type=jnp.float32)


def mdot(left, right):
    return jnp.dot(left, right, preferred_element_type=jnp.float32)


def ndot(left, right):
    return lax.dot_general(
        left, right, (((1,), (1,)), ((), ())), preferred_element_type=jnp.float32
    )


def split_heads(packed, which):
    width_all = packed.shape[1] // 3
    return packed[:, which * width_all : (which + 1) * width_all].reshape(packed.shape[0], -1, HEAD)


def scores_of(packed, segment):
    raw = product("qhd,khd->hqk", split_heads(packed, 0), split_heads(packed, 1)) * (
        1.0 / math.sqrt(HEAD)
    )
    position = jnp.arange(packed.shape[0], dtype=jnp.int32)
    allowed = (segment[:, None] == segment[None, :]) & (position[None, :] <= position[:, None])
    return jnp.where(allowed[None], raw, -jnp.inf)


def attend_back(packed, grad_mixed, logsum, segment):
    count = packed.shape[0]
    scores = scores_of(packed, segment)
    back_probs = jnp.exp(scores - logsum)
    probs_low = back_probs.astype(jnp.bfloat16)
    upstream = grad_mixed.reshape(count, -1, HEAD)
    grad_values = product("hqk,qhd->khd", probs_low, upstream)
    grad_probs = product("qhd,khd->hqk", upstream, split_heads(packed, 2))
    delta = jnp.sum(back_probs * grad_probs, axis=-1, keepdims=True)
    grad_scores = (back_probs * (grad_probs - delta) * (1.0 / math.sqrt(HEAD))).astype(jnp.bfloat16)
    grad_query = product("hqk,khd->qhd", grad_scores, split_heads(packed, 1))
    grad_keys = product("hqk,qhd->khd", grad_scores, split_heads(packed, 0))
    return jnp.concatenate(
        [
            grad_query.reshape(count, -1),
            grad_keys.reshape(count, -1),
            grad_values.reshape(count, -1),
        ],
        axis=1,
    )


class Links:
    def __init__(self, mesh):
        self.shards = mesh.shape["shard"]
        self.count = mesh.shape["replica"]
        n = self.count
        self.order = list(range(0, n, 2)) + list(range(n - 1, 0, -2))

    def xor(self, shard_bits, replica_bits):
        n = self.count
        return [
            (s * n + r, (s ^ shard_bits) * n + (r ^ replica_bits))
            for s in range(self.shards)
            for r in range(n)
        ]

    def ring(self, way):
        n = self.count
        return [
            (s * n + self.order[i], s * n + self.order[(i + way) % n])
            for s in range(self.shards)
            for i in range(n)
        ]

    def move(self, value, shard_bits, replica_bits):
        return lax.ppermute(value, AXES, self.xor(shard_bits, replica_bits))

    def place(self):
        replica = lax.axis_index("replica")
        half = replica // 2
        return jnp.where(replica % 2 == 0, half, self.count - 1 - half)


def gather_weight(links, weight, shard, quarter):
    rows, width = weight.shape
    tiles = rows // SUB
    mine = weight.reshape(tiles, SUB, width)
    size = -(-tiles // 4)
    cut = size // 2

    def start(index):
        return (index * tiles) // 4

    piece = lax.dynamic_slice_in_dim(mine, start(quarter), size, 0)
    own = links.move(piece, 2, 0)
    side = links.move(own, 0, 1)
    up = links.move(own, 0, 2)
    far_low = links.move(up[:cut], 0, 1)
    far_high = links.move(side[cut:], 0, 2)
    partner = links.move(mine, 1, 0)
    other = jnp.zeros_like(mine)
    other = lax.dynamic_update_slice_in_dim(other, own, start(quarter), 0)
    other = lax.dynamic_update_slice_in_dim(other, side, start(quarter ^ 1), 0)
    other = lax.dynamic_update_slice_in_dim(other, up, start(quarter ^ 2), 0)
    other = lax.dynamic_update_slice_in_dim(other, far_low, start(quarter ^ 3), 0)
    other = lax.dynamic_update_slice_in_dim(other, far_high, start(quarter ^ 3) + cut, 0)
    across = links.move(other, 1, 0)
    whole = jnp.zeros((links.shards,) + mine.shape, mine.dtype)
    for bits, block in ((0, mine), (1, partner), (2, other), (3, across)):
        whole = lax.dynamic_update_index_in_dim(whole, block, shard ^ bits, 0)
    return whole.reshape(links.shards * rows, width)


def gather_small(links, vectors, shard):
    sizes = [v.shape[0] for v in vectors]
    flat = jnp.concatenate(vectors)
    total = flat.shape[0]
    padded = -(-total // (SUB * 2 * LANES)) * (SUB * 2 * LANES)
    flat = jnp.pad(flat, (0, padded - total)).reshape(-1, LANES)
    whole = jnp.zeros((links.shards,) + flat.shape, flat.dtype)
    for bits in range(links.shards):
        block = flat if bits == 0 else links.move(flat, bits, 0)
        whole = lax.dynamic_update_index_in_dim(whole, block, shard ^ bits, 0)
    whole = whole.reshape(links.shards, -1)
    outs = []
    at = 0
    for size in sizes:
        outs.append(whole[:, at : at + size].reshape(-1))
        at += size
    return outs


def group_tokens(links, left, right, shard):
    tokens = left.shape[0]
    blocks = left.T.reshape(links.shards, -1, tokens)
    lefts = []
    rights = [right]
    for bits in range(links.shards):
        block = lax.dynamic_index_in_dim(blocks, shard ^ bits, 0, False)
        lefts.append(block if bits == 0 else links.move(block, bits, 0))
    near = links.move(right, 2, 0)
    rights.append(links.move(right, 1, 0))
    rights.append(near)
    rights.append(links.move(near, 1, 0))
    return jnp.concatenate(lefts, axis=1), jnp.concatenate(rights, axis=0)


def to_tiles(grad):
    rows, width = grad.shape
    wide = -(-width // LANES) * LANES
    if wide != width:
        grad = jnp.pad(grad, ((0, 0), (0, wide - width)))
    return (
        grad.reshape(rows // SUB, SUB, wide // LANES, LANES)
        .transpose(0, 2, 1, 3)
        .reshape(-1, SUB, LANES)
    )


def from_tiles(tiles, rows, width):
    wide = -(-width // LANES) * LANES
    out = (
        tiles.reshape(rows // SUB, wide // LANES, SUB, LANES)
        .transpose(0, 2, 1, 3)
        .reshape(rows, wide)
    )
    return out[:, :width] if wide != width else out


def ring_sum(links, tiles, place):
    count = links.count
    total = tiles.shape[0]
    size = -(-total // (2 * count))
    padded = jnp.pad(tiles, ((0, 2 * count * size - total), (0, 0), (0, 0)))
    ways = (1, -1)
    bases = (0, count)

    def start(way, base, step):
        return (base + (place - way * step) % count) * size

    held = [
        lax.dynamic_slice_in_dim(padded, start(w, b, 0), size, 0) for w, b in zip(ways, bases)
    ]
    for step in range(1, count):
        came = [lax.ppermute(h, AXES, links.ring(w)) for h, w in zip(held, ways)]
        held = [
            c + lax.dynamic_slice_in_dim(padded, start(w, b, step), size, 0)
            for c, w, b in zip(came, ways, bases)
        ]
    out = jnp.zeros((2 * count * size,) + tiles.shape[1:], jnp.float32)
    for step in range(count):
        for index, (w, b) in enumerate(zip(ways, bases)):
            out = lax.dynamic_update_slice_in_dim(
                out, held[index].astype(jnp.float32), start(w, b, step - 1), 0
            )
        if step < count - 1:
            held = [lax.ppermute(h, AXES, links.ring(w)) for h, w in zip(held, ways)]
    return out[:total]


def all_sum(links, value):
    bit = 1
    while bit < links.shards:
        value = value + links.move(value, bit, 0)
        bit *= 2
    bit = 1
    while bit < links.count:
        value = value + links.move(value, 0, bit)
        bit *= 2
    return value


def solution(mesh):
    links = Links(mesh)

    def local(
        layer_input,
        norm1_gain,
        norm1_shift,
        qkv_weight,
        query_bias,
        value_bias,
        out_weight,
        out_bias,
        norm2_gain,
        norm2_shift,
        fc_weight,
        fc_bias,
        proj_weight,
        proj_bias,
        cotangent,
        seq_lengths,
        seq_device,
        seq_offset,
    ):
        f32 = jnp.float32
        low = jnp.bfloat16
        count = layer_input.shape[0]
        shard = lax.axis_index("shard")
        replica = lax.axis_index("replica")
        quarter = replica % 4
        place = links.place()
        device = shard * links.count + replica
        segment, filled = segment_ids(seq_lengths, seq_device, seq_offset, device, count)

        gain1, shift1, b_query, b_value, b_out, gain2, shift2, b_fc, b_proj = [
            v.astype(f32)
            for v in gather_small(
                links,
                [
                    norm1_gain,
                    norm1_shift,
                    query_bias,
                    value_bias,
                    out_bias,
                    norm2_gain,
                    norm2_shift,
                    fc_bias,
                    proj_bias,
                ],
                shard,
            )
        ]
        w_qkv = gather_weight(links, qkv_weight, shard, quarter)
        w_out = gather_weight(links, out_weight, shard, quarter)
        w_fc = gather_weight(links, fc_weight, shard, quarter)
        w_proj = gather_weight(links, proj_weight, shard, quarter)

        inputs = layer_input.astype(f32)
        normed1, inverse1 = normalize(inputs)
        normed_in = (normed1 * gain1 + shift1).astype(low)
        bias_all = jnp.concatenate([b_query, jnp.zeros_like(b_query), b_value])
        packed = (mdot(normed_in, w_qkv) + bias_all).astype(low)
        scores = scores_of(packed, segment)
        highest = jnp.max(scores, axis=-1, keepdims=True)
        expo = jnp.exp(scores - highest)
        total = jnp.sum(expo, axis=-1, keepdims=True)
        probs = (expo / total).astype(low)
        logsum = highest + jnp.log(total)
        mixed = (
            product("hqk,khd->qhd", probs, split_heads(packed, 2)).reshape(count, -1).astype(low)
        )
        hidden = inputs + mdot(mixed, w_out) + b_out
        normed2, inverse2 = normalize(hidden)
        mlp_in = (normed2 * gain2 + shift2).astype(low)
        pre_act = mdot(mlp_in, w_fc) + b_fc
        value, slope = gelu_pair(pre_act)
        activ = value.astype(low)
        result = (hidden + mdot(activ, w_proj) + b_proj).astype(low)

        upstream = jnp.where(filled[:, None], cotangent.astype(f32), 0.0)
        upstream_low = upstream.astype(low)
        left, right = group_tokens(links, activ, upstream_low, shard)
        grad_wproj = mdot(left, right).astype(low)
        sum_wproj = ring_sum(links, to_tiles(grad_wproj), place)

        grad_pre = ndot(upstream_low, w_proj) * slope
        grad_pre_low = grad_pre.astype(low)
        left, right = group_tokens(links, mlp_in, grad_pre_low, shard)
        grad_wfc = mdot(left, right).astype(low)
        sum_wfc = ring_sum(links, to_tiles(grad_wfc), place)

        grad_mlp_in = ndot(grad_pre_low, w_fc)
        grad_hidden = upstream + norm_back(grad_mlp_in * gain2, normed2, inverse2)
        grad_hidden_low = grad_hidden.astype(low)
        left, right = group_tokens(links, mixed, grad_hidden_low, shard)
        grad_wout = mdot(left, right).astype(low)

        grad_mixed = ndot(grad_hidden_low, w_out).astype(low)
        grad_packed = attend_back(packed, grad_mixed, logsum, segment)
        grad_packed_low = grad_packed.astype(low)
        left, right = group_tokens(links, normed_in, grad_packed_low, shard)
        grad_wqkv = mdot(left, right).astype(low)
        tiles_out = to_tiles(grad_wout)
        tiles_qkv = to_tiles(grad_wqkv)
        both = ring_sum(links, jnp.concatenate([tiles_out, tiles_qkv], axis=0), place)
        sum_wout = both[: tiles_out.shape[0]]
        sum_wqkv = both[tiles_out.shape[0] :]

        grad_in = ndot(grad_packed_low, w_qkv)
        grad_inputs = (grad_hidden + norm_back(grad_in * gain1, normed1, inverse1)).astype(low)

        width = gain1.shape[0]
        vectors = [
            jnp.sum(grad_in * normed1, axis=0),
            jnp.sum(grad_in, axis=0),
            jnp.sum(grad_packed[:, :width], axis=0),
            jnp.sum(grad_packed[:, 2 * width :], axis=0),
            jnp.sum(grad_hidden, axis=0),
            jnp.sum(grad_mlp_in * normed2, axis=0),
            jnp.sum(grad_mlp_in, axis=0),
            jnp.sum(grad_pre, axis=0),
            jnp.sum(upstream, axis=0),
        ]
        sizes = [v.shape[0] for v in vectors]
        flat = jnp.concatenate(vectors)
        wide = -(-flat.shape[0] // (SUB * LANES)) * SUB * LANES
        flat = jnp.pad(flat, (0, wide - flat.shape[0])).reshape(-1, LANES)
        flat = all_sum(links, flat).reshape(-1)
        sums = []
        at = 0
        for size in sizes:
            part = flat[at : at + size].reshape(links.shards, -1)
            sums.append(lax.dynamic_index_in_dim(part, shard, 0, False))
            at += size

        return (
            result,
            grad_inputs,
            sums[0],
            sums[1],
            from_tiles(sum_wqkv, *qkv_weight.shape),
            sums[2],
            sums[3],
            from_tiles(sum_wout, *out_weight.shape),
            sums[4],
            sums[5],
            sums[6],
            from_tiles(sum_wfc, *fc_weight.shape),
            sums[7],
            from_tiles(sum_wproj, *proj_weight.shape),
            sums[8],
        )

    rows = P("shard", None)
    vector = P("shard")
    tokens = P(("shard", "replica"), None)
    return jax.shard_map(
        local,
        mesh=mesh,
        in_specs=(
            tokens,
            vector,
            vector,
            rows,
            vector,
            vector,
            rows,
            vector,
            vector,
            vector,
            rows,
            vector,
            rows,
            vector,
            tokens,
            P(),
            P(),
            P(),
        ),
        out_specs=(
            tokens,
            tokens,
            vector,
            vector,
            rows,
            vector,
            vector,
            rows,
            vector,
            vector,
            vector,
            rows,
            vector,
            rows,
            vector,
        ),
        check_vma=False,
    )
```
